32 devices in a mesh: dp: 4 (over y, x), expert: 8 (over z, core).
Axes of the slice: x: 2, y: 2, z: 4, core: 2. Of those that a mesh axis runs over, the one named last changes fastest.
Arguments:
- tokens: bfloat16 [4096, 1536], P('expert'), may hold values from -6 to 6
- past_len: int32 [32], P('expert'), may hold values from 1 to 4608
- cache_keys: bfloat16 [32, 4608, 512], P('expert', None, 'dp'), may hold values from -32 to 32
- cache_values: bfloat16 [32, 4608, 512], P('expert', None, 'dp'), may hold values from -6 to 6
- attn_gain: float32 [1536], replicated, may hold values from 0.1 to 1.9
- w_query: bfloat16 [1536, 1536], P(None, 'dp'), may hold values from -3 to 3
- w_key: bfloat16 [1536, 512], P(None, 'dp'), may hold values from -0.15625 to 0.15625
- w_value: bfloat16 [1536, 512], P(None, 'dp'), may hold values from -0.15625 to 0.15625
- w_out: bfloat16 [1536, 1536], P('dp'), may hold values from -0.15625 to 0.15625
- moe_gain: float32 [1536], replicated, may hold values from 0.1 to 1.9
- router: bfloat16 [1536, 40], replicated, may hold values from -16 to 16
- expert_in: bfloat16 [64, 1536, 1024], P('expert'), may hold values from -0.15625 to 0.15625
- expert_out: bfloat16 [64, 512, 1536], P('expert'), may hold values from -1 to 1
- final_gain: float32 [1536], replicated, may hold values from 0.1 to 1.9
- slot_owner: int32 [64], replicated, may hold values from 0 to 39, as said below
- routes: int32 [4096, 8], P(('expert', 'dp')), may hold values from 0 to 39, all different within a row; in each aligned block of 128 rows (0 to 127, 128 to 255, ...) at most 40 rows name the same one
- split_pick: int32 [4096, 8], P(('expert', 'dp')), may hold values from 0 to 2519
Outputs:
- output: bfloat16 [4096, 1536], P(('expert', 'dp'))
The draws below stay inside these ranges and needn't reach their ends.
Inputs may be any that keep to these rules, and one draw needn't show every extreme that they name: `routes`: each row names 8 different experts; at most 40 rows of one device name one expert, a bound that some block reaches. `slot_owner`: every expert is served by at least one slot.
All inputs are finite; a program needn't handle non-finite values.
Results may differ from the reference program's by a relative error of at most 0.025.
Values may be sent and summed in bfloat16 or wider, within the bound.
A program may use at most 128 MiB of HBM per device.

```python
import math
import jax
import jax.numpy as jnp
import numpy as np
from jax import lax

D = 1536
HEADS = 24
KVH = 8
HD = 64
EXPERTS = 40
FF = 512
TOPK = 8
SINK = 4
WINDOW = 4096
CAP = 4608
QPR = 128
TOK_DEV = 128
TOKENS = 4096
REQS = 32
SLOTS = 64
MOST = 40


def draw_w_query(key, part):
    noise = jnp.clip(jax.random.normal(jax.random.fold_in(key, 11), (D, HEADS * HD), jnp.float32), -6.0, 6.0) / math.sqrt(D)
    return noise.astype(jnp.bfloat16)


def draw_cache_keys(key, part):
    noise = jnp.clip(jax.random.normal(jax.random.fold_in(key, 21), (REQS, CAP, KVH * HD), jnp.float32), -6.0, 6.0)
    return noise.astype(jnp.bfloat16)


def draw_router(key, part):
    noise = jnp.clip(jax.random.normal(jax.random.fold_in(key, 31), (D, EXPERTS), jnp.float32), -6.0, 6.0)
    values = 0.35 * noise / math.sqrt(D)
    return values.astype(jnp.bfloat16)


def draw_slot_owner(key, part):
    order = jax.random.permutation(jax.random.fold_in(key, 41), SLOTS)
    extra = jax.random.randint(jax.random.fold_in(key, 42), (SLOTS,), 0, EXPERTS)
    return jnp.where(order < EXPERTS, order, extra).astype(jnp.int32)


def with_ends(array, own_key, smallest, top_value):
    dims = array.shape
    place = [jax.random.randint(jax.random.fold_in(own_key, axis), (), 0, dims[axis]) for axis in range(len(dims))]
    array = array.at[tuple(place)].set(smallest)
    longest = dims.index(max(dims))
    place[longest] = (place[longest] + 1) % dims[longest]
    return array.at[tuple(place)].set(top_value)


def levels(stream_key, shape, cuts, smallest, top_value):
    level, own = 1.0, jax.random.fold_in(stream_key, 6)
    for dim, parts in cuts:
        steps = jnp.exp(jax.random.uniform(jax.random.fold_in(own, dim), (parts,), jnp.float32, smallest / len(cuts), top_value / len(cuts)))
        level = level * jnp.repeat(steps, shape[dim] // parts).reshape([-1 if axis == dim else 1 for axis in range(len(shape))])
    return level


def routed_block(key, own, number, rows, amount, top, most, lean):
    ranking = jax.random.permutation(key, amount)
    packed, ordinary = load_shares(amount, rows * top, most, lean, True), load_shares(amount, rows * top, most, lean, False)
    places = jnp.arange(amount)

    def named(lengths, offset_by):
        used = int((lengths > 0).sum())
        fixed = max(1, used // 4)
        moved = fixed + (places - fixed + offset_by * (used - fixed)) % max(1, amount - fixed)
        return jnp.zeros((amount,), jnp.int32).at[ranking[jnp.where(places < fixed, places, moved)]].set(jnp.asarray(lengths, jnp.int32))

    lengths = jnp.where(number % 4 == 0, named(packed, number // 4), named(ordinary, number - number // 4 - 1))
    mixed = jax.random.permutation(jax.random.fold_in(own, 3), amount)
    giver, sink = mixed[0:amount // 2 * 2:2], mixed[1:amount // 2 * 2:2]
    margin = jnp.minimum(lengths[giver] - 1, most - lengths[sink]) // 2
    margin = jnp.where((giver == ranking[0]) | (sink == ranking[0]) | (lengths[sink] == 0), 0, jnp.maximum(margin, 0))
    moved = jax.random.randint(jax.random.fold_in(own, 4), (amount // 2,), 0, 1 << 20) % (margin + 1)
    lengths = lengths.at[giver].add(-moved).at[sink].add(moved)
    members = jnp.searchsorted(jnp.cumsum(lengths), jnp.arange(rows * top), side="right").astype(jnp.int32)
    grid = members.reshape(top, rows).T
    grid = grid[jax.random.permutation(jax.random.fold_in(own, 1), rows)]
    offset_by = jax.random.randint(jax.random.fold_in(own, 2), (rows, 1), 0, top)
    return jnp.take_along_axis(grid, (jnp.arange(top)[None, :] + offset_by) % top, axis=1)


def load_shares(number_of, total, bound, slope, full):
    portions = [(1 << 20) // math.isqrt(rank ** slope) + 1 for rank in range(1, number_of + 1)]
    largest = bound if full else min(bound, max(-(-total // number_of), total * portions[0] // sum(portions)))
    least = 1 if total - largest >= number_of - 1 else 0
    given, spare = [largest] + [least] * (number_of - 1), total - largest - least * (number_of - 1)
    while spare > 0:
        movable = [i for i in range(1, number_of) if given[i] < largest] or [i for i in range(1, number_of) if given[i] < bound]
        pool, budget = sum([portions[i] for i in movable]), spare
        for i in movable:
            more = min(bound - given[i], max(1, budget * portions[i] // pool), spare)
            given[i] = given[i] + more
            spare = spare - more
    return np.array(given)


def scatter_about(key, dims, deviation, bound, shards=(), kind=jnp.bfloat16):
    loudness = levels(key, dims, shards, -0.22, 0.18) if shards else 1.0
    entries = jax.random.normal(key, dims, jnp.float32) * deviation * loudness
    return jnp.minimum(jnp.maximum(entries, -bound), bound).astype(kind)


def setup_inputs(seed: int = 0) -> dict:
    seeds = jax.random.split(jax.random.key(seed), 18)
    tokens = scatter_about(seeds[0], (TOKENS, D), 1.0, 6.0, ((0, 8),))
    past_len = with_ends(jax.random.randint(seeds[1], (REQS,), 1, CAP + 1), jax.random.fold_in(seeds[1], 1), 1, CAP).astype(jnp.int32)
    cache_keys = draw_cache_keys(jax.random.fold_in(seeds[17], 71), 0)
    cache_values = scatter_about(seeds[3], (REQS, CAP, KVH * HD), 1.0, 6.0, ((0, 8), (2, 4)))
    attn_gain = jnp.clip(1.0 + 0.18 * jax.random.normal(seeds[4], (D,), jnp.float32), 0.1, 1.9)
    w_query = draw_w_query(jax.random.fold_in(seeds[17], 71), 0)
    w_key = scatter_about(seeds[6], (D, KVH * HD), D ** -0.5, 0.15625, ((1, 4),))
    w_value = scatter_about(seeds[7], (D, KVH * HD), D ** -0.5, 0.15625, ((1, 4),))
    w_out = scatter_about(seeds[8], (HEADS * HD, D), (HEADS * HD) ** -0.5, 0.15625, ((0, 4),))
    moe_gain = jnp.clip(1.0 + 0.18 * jax.random.normal(seeds[9], (D,), jnp.float32), 0.1, 1.9)
    router = draw_router(jax.random.fold_in(seeds[17], 71), 0)
    expert_in = scatter_about(seeds[11], (SLOTS, D, 2 * FF), D ** -0.5, 0.15625, ((0, 8),))
    expert_out = scatter_about(seeds[12], (SLOTS, FF, D), (FF // 16) ** -0.5, 1.0, ((0, 8),))
    final_gain = jnp.clip(1.0 + 0.18 * jax.random.normal(seeds[13], (D,), jnp.float32), 0.1, 1.9)
    slot_owner = draw_slot_owner(jax.random.fold_in(seeds[17], 71), 0)
    routes_keys = jax.random.split(jax.random.fold_in(seeds[15], 1), TOKENS // TOK_DEV)
    routes_turns = jax.random.permutation(jax.random.fold_in(seeds[15], 3), TOKENS // TOK_DEV)
    routes = jax.vmap(lambda own, number: routed_block(jax.random.fold_in(seeds[15], 2), own, number, TOK_DEV, EXPERTS, TOPK, MOST, 2))(routes_keys, routes_turns).reshape((TOKENS, TOPK))
    split_pick = with_ends(jax.random.randint(seeds[16], (TOKENS, TOPK), 0, 2520), jax.random.fold_in(seeds[16], 1), 0, 2519).astype(jnp.int32)
    return {"tokens": tokens, "past_len": past_len, "cache_keys": cache_keys, "cache_values": cache_values, "attn_gain": attn_gain, "w_query": w_query, "w_key": w_key, "w_value": w_value, "w_out": w_out, "moe_gain": moe_gain, "router": router, "expert_in": expert_in, "expert_out": expert_out, "final_gain": final_gain, "slot_owner": slot_owner, "routes": routes, "split_pick": split_pick}


epsilon = 1e-05

def rms_scale(values, gain):
    widened = values.astype(jnp.float32)
    mean_square = lax.optimization_barrier(jnp.mean(widened * widened, axis=-1, keepdims=True))
    return widened * lax.rsqrt(mean_square + epsilon) * gain.astype(jnp.float32)

def attend_request(item):
    queries, keys_new, values_new, keys_past, values_past, length = item
    share_count = HEADS // KVH
    query_all = queries.astype(jnp.float32).reshape(QPR, KVH, share_count, HD)
    keys_all = jnp.concatenate([keys_past.reshape(CAP, KVH, HD), keys_new.reshape(QPR, KVH, HD)], 0).astype(jnp.float32)
    values_all = jnp.concatenate([values_past.reshape(CAP, KVH, HD), values_new.reshape(QPR, KVH, HD)], 0).astype(jnp.float32)
    scores = jnp.einsum('qkgd,pkd->kgqp', query_all, keys_all) * HD ** (-0.5)
    position = jnp.arange(QPR, dtype=jnp.int32)[:, None]
    slot_place = jnp.arange(CAP, dtype=jnp.int32)[None, :]
    live_past = (slot_place < length) & ((slot_place < SINK) | (slot_place >= length + position - WINDOW + 1))
    live_new = jnp.arange(QPR, dtype=jnp.int32)[None, :] <= position
    live = jnp.concatenate([live_past, live_new], 1)
    masked = jnp.where(live, scores, -jnp.inf)
    highest = lax.optimization_barrier(jnp.max(masked, axis=-1, keepdims=True))
    weights = jnp.where(live, jnp.exp(masked - highest), 0.0)
    totals = lax.optimization_barrier(jnp.sum(weights, axis=-1, keepdims=True))
    rounded = lax.optimization_barrier(weights.astype(jnp.bfloat16))
    summed = jnp.einsum('kgqp,pkd->kgqd', rounded.astype(jnp.float32), values_all) / totals
    return summed.transpose(2, 0, 1, 3).reshape(QPR, HEADS * HD).astype(jnp.bfloat16)

def reference(tokens, past_len, cache_keys, cache_values, attn_gain, w_query, w_key, w_value, w_out, moe_gain, router, expert_in, expert_out, final_gain, slot_owner, routes, split_pick):
    normed = rms_scale(tokens, attn_gain).astype(jnp.bfloat16)
    queries = jnp.dot(normed, w_query, preferred_element_type=jnp.float32).astype(jnp.bfloat16)
    keys_new = jnp.dot(normed, w_key, preferred_element_type=jnp.float32).astype(jnp.bfloat16)
    values_new = jnp.dot(normed, w_value, preferred_element_type=jnp.float32).astype(jnp.bfloat16)
    heads = lax.map(attend_request, (queries.reshape(REQS, QPR, HEADS * HD), keys_new.reshape(REQS, QPR, KVH * HD), values_new.reshape(REQS, QPR, KVH * HD), cache_keys, cache_values, past_len))
    heads = heads.reshape(TOKENS, HEADS * HD)
    stream = tokens.astype(jnp.float32) + jnp.dot(heads, w_out, preferred_element_type=jnp.float32)
    moe_in = rms_scale(stream, moe_gain).astype(jnp.bfloat16)
    logits = jnp.dot(moe_in, router, preferred_element_type=jnp.float32)
    chosen = jnp.take_along_axis(logits, routes, axis=1)
    gates = jax.nn.softmax(chosen, axis=-1)
    slot_ids = jnp.arange(SLOTS, dtype=jnp.int32)
    same_owner = slot_owner[:, None] == slot_owner[None, :]
    slot_rank = lax.optimization_barrier(jnp.sum((same_owner & (slot_ids[None, :] < slot_ids[:, None])).astype(jnp.int32), axis=1))
    serving = slot_owner[None, None, :] == routes[:, :, None]
    replicas = lax.optimization_barrier(jnp.sum(serving.astype(jnp.int32), axis=-1))
    wanted = split_pick % replicas
    target = lax.optimization_barrier(jnp.sum(jnp.where(serving & (slot_rank[None, None, :] == wanted[:, :, None]), slot_ids[None, None, :], 0), axis=-1)).astype(jnp.int32)
    route_count = TOKENS * TOPK
    flat_slot = target.reshape(route_count)
    tile_rows = 128
    tiles = (route_count + tile_rows - 1) // tile_rows + SLOTS
    counts = lax.optimization_barrier(jnp.sum((flat_slot[:, None] == slot_ids[None, :]).astype(jnp.int32), axis=0))
    padded = (counts + tile_rows - 1) // tile_rows * tile_rows
    starts = jnp.cumsum(padded) - padded
    firsts = jnp.cumsum(counts) - counts
    order = jnp.argsort(flat_slot, stable=True).astype(jnp.int32)
    sorted_slot = flat_slot[order]
    placed = (starts[sorted_slot] + jnp.arange(route_count, dtype=jnp.int32) - firsts[sorted_slot]).astype(jnp.int32)
    location = jnp.zeros((route_count,), jnp.int32).at[order].set(placed)
    source_index = (jnp.arange(route_count, dtype=jnp.int32) // TOPK).astype(jnp.int32)
    buffer = jnp.zeros((tiles * tile_rows, D), jnp.bfloat16).at[location].set(moe_in[source_index])
    ends = starts + padded
    tile_start = jnp.arange(tiles, dtype=jnp.int32) * tile_rows
    tile_slot = jnp.minimum(lax.optimization_barrier(jnp.sum((ends[None, :] <= tile_start[:, None]).astype(jnp.int32), axis=1)), SLOTS - 1).astype(jnp.int32)

    def run_tile(item):
        tile_in, which = item
        gate_up = jnp.dot(tile_in, expert_in[which], preferred_element_type=jnp.float32)
        activation = (jax.nn.silu(gate_up[:, :FF]) * gate_up[:, FF:]).astype(jnp.bfloat16)
        return jnp.dot(activation, expert_out[which], preferred_element_type=jnp.float32).astype(jnp.bfloat16)
    outputs = lax.map(run_tile, (buffer.reshape(tiles, tile_rows, D), tile_slot)).reshape(tiles * tile_rows, D)
    expert_rows = outputs[location].reshape(TOKENS, TOPK, D)
    combined = stream + lax.optimization_barrier(jnp.sum(gates[:, :, None] * expert_rows.astype(jnp.float32), axis=1))
    return rms_scale(combined, final_gain).astype(jnp.bfloat16)
```

```python
import functools
import math

import jax
import jax.numpy as jnp
from jax import lax
from jax.experimental import pallas as pl
from jax.experimental.pallas import tpu as pltpu
from jax.sharding import PartitionSpec as P

HD = 64
SINK = 4
WINDOW = 4096
MOST_ROWS = 2048

epsilon = 1e-05
neg_large = -1e30


def rms_scale(values, gain):
    widened = values.astype(jnp.float32)
    mean_square = jnp.mean(widened * widened, axis=-1, keepdims=True)
    return widened * lax.rsqrt(mean_square + epsilon) * gain


def mm(a, b):
    return jnp.dot(a, b, preferred_element_type=jnp.float32)


def attend_kernel(
    key_block, len_ref, tok_ref, gain_ref, wq_ref, wk_ref, wv_ref, wo_ref, kc_ref, vc_ref,
    out_ref, qt_ref, top_ref, total_ref, acc_ref,
):
    length = len_ref[pl.program_id(0)]
    rows = tok_ref.shape[0]
    heads = wq_ref.shape[1] // HD
    kv_local = wk_ref.shape[1] // HD
    share = heads // kv_local
    columns = heads * rows
    normed = rms_scale(tok_ref[...], gain_ref[...]).astype(jnp.bfloat16)
    queries = mm(normed, wq_ref[...]).astype(jnp.bfloat16).astype(jnp.float32) * HD ** (-0.5)
    queries_t = queries.T.astype(jnp.bfloat16)
    qt_ref[...] = jnp.zeros_like(qt_ref)
    for h in range(heads):
        kv = h // share
        qt_ref[kv * HD : (kv + 1) * HD, h * rows : (h + 1) * rows] = queries_t[h * HD : (h + 1) * HD, :]
    keys_new = mm(normed, wk_ref[...]).astype(jnp.bfloat16)
    values_new = mm(normed, wv_ref[...]).astype(jnp.bfloat16)

    def weigh(values, weights):
        return lax.dot_general(
            values, weights, (((0,), (0,)), ((), ())), preferred_element_type=jnp.float32
        )

    scores = mm(keys_new, qt_ref[...])
    key_pos = lax.broadcasted_iota(jnp.int32, (rows, columns), 0)
    query_pos = lax.broadcasted_iota(jnp.int32, (rows, columns), 1) % rows
    scores = jnp.where(key_pos <= query_pos, scores, neg_large)
    top = jnp.max(scores, axis=0, keepdims=True)
    weights = jnp.exp(scores - top)
    top_ref[...] = top
    total_ref[...] = jnp.sum(weights, axis=0, keepdims=True)
    acc_ref[...] = weigh(values_new, weights.astype(jnp.bfloat16))

    def visit(block_idx, masked):
        start = pl.multiple_of(block_idx * key_block, key_block)
        scores = mm(kc_ref[0, pl.ds(start, key_block), :], qt_ref[...])
        if masked:
            place = start + lax.broadcasted_iota(jnp.int32, (key_block, columns), 0)
            first = length - WINDOW + 1 + lax.broadcasted_iota(jnp.int32, (1, columns), 1) % rows
            live = (place < length) & ((place < SINK) | (place >= first))
            scores = jnp.where(live, scores, neg_large)
        top_old = top_ref[...]
        top_new = jnp.maximum(top_old, jnp.max(scores, axis=0, keepdims=True))
        weights = jnp.exp(scores - top_new)
        factor = jnp.exp(top_old - top_new)
        top_ref[...] = top_new
        total_ref[...] = total_ref[...] * factor + jnp.sum(weights, axis=0, keepdims=True)
        acc_ref[...] = acc_ref[...] * factor + weigh(
            vc_ref[0, pl.ds(start, key_block), :], weights.astype(jnp.bfloat16)
        )

    blocks = (length + key_block - 1) // key_block
    low = jnp.minimum(
        (jnp.maximum(length + rows - WINDOW, 0) + key_block - 1) // key_block, blocks
    )
    high = jnp.maximum(low, length // key_block)

    def run(begin, end, masked):
        def step(block_idx, carried):
            visit(block_idx, masked)
            return carried

        lax.fori_loop(begin, end, step, 0)

    run(0, low, True)
    run(low, high, False)
    run(high, blocks, True)
    result = acc_ref[...] / total_ref[...]
    parts = []
    for h in range(heads):
        kv = h // share
        parts.append(result[kv * HD : (kv + 1) * HD, h * rows : (h + 1) * rows])
    heads_rows = jnp.concatenate(parts, axis=0).T.astype(jnp.bfloat16)
    out_ref[...] = mm(heads_rows, wo_ref[...]).astype(jnp.bfloat16)


def attend(past_len, tokens, gain, w_query, w_key, w_value, w_out, cache_keys, cache_values):
    requests, capacity, kv_width = cache_keys.shape
    group_rows, width = tokens.shape
    rows = group_rows // requests
    key_block = math.gcd(capacity, 512)
    columns = w_query.shape[1] // HD * rows

    def whole(array):
        return pl.BlockSpec(
            array.shape, lambda i, lens: (0,) * array.ndim, pipeline_mode=pl.Buffered(1)
        )

    gain = gain.reshape(1, width)
    cache_spec = pl.BlockSpec((1, capacity, kv_width), lambda i, lens: (i, 0, 0))
    row_spec = pl.BlockSpec((rows, width), lambda i, lens: (i, 0))
    return pl.pallas_call(
        functools.partial(attend_kernel, key_block),
        out_shape=jax.ShapeDtypeStruct((group_rows, width), jnp.bfloat16),
        grid_spec=pltpu.PrefetchScalarGridSpec(
            num_scalar_prefetch=1,
            grid=(requests,),
            in_specs=[row_spec]
            + [whole(a) for a in (gain, w_query, w_key, w_value, w_out)]
            + [cache_spec, cache_spec],
            out_specs=row_spec,
            scratch_shapes=[
                pltpu.VMEM((kv_width, columns), jnp.bfloat16),
                pltpu.VMEM((1, columns), jnp.float32),
                pltpu.VMEM((1, columns), jnp.float32),
                pltpu.VMEM((kv_width, columns), jnp.float32),
            ],
        ),
        compiler_params=pltpu.CompilerParams(vmem_limit_bytes=48 << 20),
        name="attend",
    )(past_len, tokens, gain, w_query, w_key, w_value, w_out, cache_keys, cache_values)


def gate_kernel(attn_ref, tok_ref, gain_ref, router_ref, chosen_ref, stream_ref, ext_ref):
    width = tok_ref.shape[1]
    stream = tok_ref[...].astype(jnp.float32) + attn_ref[...].astype(jnp.float32)
    stream_ref[...] = stream
    moe_in = rms_scale(stream, gain_ref[...]).astype(jnp.bfloat16)
    ext_ref[:, :width] = moe_in
    logits = mm(moe_in, router_ref[...])
    chosen = chosen_ref[...] > 0.0
    top = jnp.max(jnp.where(chosen, logits, neg_large), axis=-1, keepdims=True)
    weights = jnp.where(chosen, jnp.exp(jnp.where(chosen, logits, top) - top), 0.0)
    gates = weights / (0.5 * jnp.sum(weights, axis=-1, keepdims=True))
    half = gates.shape[1] // 2
    coarse = gates.astype(jnp.bfloat16).astype(jnp.float32)
    lane = lax.broadcasted_iota(jnp.int32, gates.shape, 1)
    ext_ref[:, width:] = jnp.where(lane < half, coarse, gates - coarse).astype(jnp.bfloat16)


def gate_rows(attn_rows, rows_mine, gain, router2, chosen2):
    rows, width = rows_mine.shape
    return pl.pallas_call(
        gate_kernel,
        out_shape=(
            jax.ShapeDtypeStruct((rows, width), jnp.float32),
            jax.ShapeDtypeStruct((rows, width + router2.shape[1]), jnp.bfloat16),
        ),
        name="gate_rows",
    )(attn_rows, rows_mine, gain.reshape(1, width), router2, chosen2)


def experts_kernel(
    span, me_ref, ext_ref, win_ref, wout_ref, out_ref, rank_ref, rank_t_ref, acc_ref
):
    s = pl.program_id(0)
    slots = pl.num_programs(0)
    rows, wide = ext_ref.shape
    width = acc_ref.shape[1]
    extra = wide - width
    ff_width = wout_ref.shape[1]
    first = me_ref[0] * slots

    def pick_slot(shape, dim_from, dim_to, offset):
        source = lax.broadcasted_iota(jnp.int32, shape, dim_from) % (extra // 2)
        target = lax.broadcasted_iota(jnp.int32, shape, dim_to)
        return source == target + offset

    @pl.when(s == 0)
    def _():
        choose = pick_slot((extra, 128), 0, 1, first) & (
            lax.broadcasted_iota(jnp.int32, (extra, 128), 1) < slots
        )
        choose = jnp.where(choose, 1.0, 0.0).astype(jnp.bfloat16)
        before = jnp.where(
            lax.broadcasted_iota(jnp.int32, (span, span), 1)
            < lax.broadcasted_iota(jnp.int32, (span, span), 0),
            1.0,
            0.0,
        ).astype(jnp.bfloat16)
        seen = jnp.zeros((1, 128), jnp.float32)
        for part in range(rows // span):
            here = slice(part * span, (part + 1) * span)
            used = mm(ext_ref[here, width:], choose) > 0.0
            ones = jnp.where(used, 1.0, 0.0)
            rank = mm(before, ones.astype(jnp.bfloat16)) + seen
            rank = jnp.where(used, rank, -1.0)
            seen = seen + jnp.sum(ones, axis=0, keepdims=True)
            rank_ref[here, :] = rank
            rank_t_ref[:, here] = rank.T[: rank_t_ref.shape[0], :]
        acc_ref[...] = jnp.zeros_like(acc_ref)

    rank_row = rank_t_ref[pl.ds(s, 1), :]
    count = jnp.max(rank_row).astype(jnp.int32) + 1
    chunk = math.gcd(rows, 512)
    tile_rows = 256 if rows <= MOST_ROWS else 64

    def tile(index, carried):
        base = (index * tile_rows).astype(jnp.float32)
        wanted = base + lax.broadcasted_iota(jnp.int32, (tile_rows, rows), 0).astype(jnp.float32)
        select = jnp.where(wanted == rank_row, 1.0, 0.0).astype(jnp.bfloat16)
        taken = mm(select, ext_ref[...])
        moe_in = taken[:, :width].astype(jnp.bfloat16)
        lane = lax.broadcasted_iota(jnp.int32, (tile_rows, extra), 1) % (extra // 2)
        mine = lane == first + s
        gate = jnp.sum(jnp.where(mine, taken[:, width:], 0.0), axis=1, keepdims=True)
        gate_up = mm(moe_in, win_ref[0])
        g = gate_up[:, :ff_width]
        activation = (g / (1.0 + jnp.exp(-g)) * gate_up[:, ff_width:]).astype(jnp.bfloat16)
        produced = (mm(activation, wout_ref[0]) * gate).astype(jnp.bfloat16)
        for part in range(rows // chunk):
            here = slice(part * chunk, (part + 1) * chunk)
            lane_id = lax.broadcasted_iota(jnp.int32, (chunk, 128), 1)
            column = jnp.sum(
                jnp.where(lane_id == s, rank_ref[here, :], 0.0), axis=1, keepdims=True
            )
            place = base + lax.broadcasted_iota(jnp.int32, (chunk, tile_rows), 1).astype(jnp.float32)
            spread = jnp.where(place == column, 1.0, 0.0).astype(jnp.bfloat16)
            acc_ref[here, :] = acc_ref[here, :] + mm(spread, produced)
        return carried

    lax.fori_loop(0, (count + tile_rows - 1) // tile_rows, tile, 0)

    @pl.when(s == slots - 1)
    def _():
        out_ref[...] = acc_ref[...].astype(jnp.bfloat16)


def run_experts(me, gathered, expert_in, expert_out, span):
    rows, wide = gathered.shape
    slots, width, double = expert_in.shape
    ff_width = expert_out.shape[1]
    return pl.pallas_call(
        functools.partial(experts_kernel, span),
        out_shape=jax.ShapeDtypeStruct((rows, width), jnp.bfloat16),
        grid_spec=pltpu.PrefetchScalarGridSpec(
            num_scalar_prefetch=1,
            grid=(slots,),
            in_specs=[
                pl.BlockSpec((rows, wide), lambda i, me: (0, 0), pipeline_mode=pl.Buffered(1)),
                pl.BlockSpec((1, width, double), lambda i, me: (i, 0, 0)),
                pl.BlockSpec((1, ff_width, width), lambda i, me: (i, 0, 0)),
            ],
            out_specs=pl.BlockSpec((rows, width), lambda i, me: (0, 0), pipeline_mode=pl.Buffered(1)),
            scratch_shapes=[
                pltpu.VMEM((rows, 128), jnp.float32),
                pltpu.VMEM((-(-slots // 8) * 8, rows), jnp.float32),
                pltpu.VMEM((rows, width), jnp.float32),
            ],
        ),
        compiler_params=pltpu.CompilerParams(vmem_limit_bytes=64000 << 10),
        name="run_experts",
    )(me, gathered, expert_in, expert_out)


def choose_slots(slot_owner, routes, split_pick):
    slot_ids = jnp.arange(slot_owner.shape[0], dtype=jnp.int32)
    same_owner = slot_owner[:, None] == slot_owner[None, :]
    slot_rank = jnp.sum(
        (same_owner & (slot_ids[None, :] < slot_ids[:, None])).astype(jnp.int32), axis=1
    )
    replicas = jnp.sum(same_owner.astype(jnp.int32), axis=1)
    hits = (slot_owner[None, None, :] == routes[:, :, None]) & (
        slot_rank[None, None, :] == split_pick[:, :, None] % replicas[None, None, :]
    )
    return jnp.any(hits, axis=1).astype(jnp.float32)


def shards(
    tokens,
    past_len,
    cache_keys,
    cache_values,
    attn_gain,
    w_query,
    w_key,
    w_value,
    w_out,
    moe_gain,
    router,
    expert_in,
    expert_out,
    final_gain,
    slot_owner,
    routes,
    split_pick,
):
    chosen = choose_slots(slot_owner, routes, split_pick)
    chosen2 = jnp.concatenate([chosen, chosen], axis=1)
    owner2 = jnp.concatenate([slot_owner, slot_owner])
    pick = owner2[None, :] == jnp.arange(router.shape[1], dtype=jnp.int32)[:, None]
    router2 = mm(router, pick.astype(jnp.bfloat16)).astype(jnp.bfloat16)
    projected = attend(
        past_len, tokens, attn_gain, w_query, w_key, w_value, w_out, cache_keys, cache_values
    )
    tok_dev = tokens.shape[0] // lax.axis_size("dp")
    attn_rows = lax.psum_scatter(projected, "dp", scatter_dimension=0, tiled=True)
    rows_mine = lax.dynamic_slice_in_dim(tokens, lax.axis_index("dp") * tok_dev, tok_dev, 0)
    stream, extended = gate_rows(attn_rows, rows_mine, moe_gain, router2, chosen2)
    gathered = lax.all_gather(extended, "expert", axis=0, tiled=True)
    me = lax.axis_index("expert").astype(jnp.int32).reshape(1)
    partial = run_experts(me, gathered, expert_in, expert_out, tok_dev)
    mixed = lax.psum_scatter(partial, "expert", scatter_dimension=0, tiled=True)
    combined = stream + mixed.astype(jnp.float32)
    return rms_scale(combined, final_gain).astype(jnp.bfloat16)


def solution(mesh):
    return jax.shard_map(
        shards,
        mesh=mesh,
        in_specs=(
            P("expert", None),
            P("expert"),
            P("expert", None, "dp"),
            P("expert", None, "dp"),
            P(),
            P(None, "dp"),
            P(None, "dp"),
            P(None, "dp"),
            P("dp", None),
            P(),
            P(),
            P("expert", None, None),
            P("expert", None, None),
            P(),
            P(),
            P(("expert", "dp"), None),
            P(("expert", "dp"), None),
        ),
        out_specs=P(("expert", "dp"), None),
        check_vma=False,
    )
```

```python
import functools
import math

import jax
import jax.numpy as jnp
from jax import lax
from jax.experimental import pallas as pl
from jax.experimental.pallas import tpu as pltpu
from jax.sharding import PartitionSpec as P

HD = 64
SINK = 4
WINDOW = 4096
MOST_ROWS = 2048
CHUNKS = 2

epsilon = 1e-05
neg_large = -1e30


def rms_scale(values, gain):
    widened = values.astype(jnp.float32)
    mean_square = jnp.mean(widened * widened, axis=-1, keepdims=True)
    return widened * lax.rsqrt(mean_square + epsilon) * gain


def mm(a, b):
    return jnp.dot(a, b, preferred_element_type=jnp.float32)


def attend_kernel(
    key_block, len_ref, tok_ref, gain_ref, wq_ref, wk_ref, wv_ref, wo_ref, kc_ref, vc_ref,
    *refs,
):
    out_refs, (qt_ref, top_ref, total_ref, acc_ref) = refs[:-4], refs[-4:]
    length = len_ref[pl.program_id(0)]
    rows = tok_ref.shape[0]
    heads = wq_ref.shape[1] // HD
    kv_local = wk_ref.shape[1] // HD
    share = heads // kv_local
    columns = heads * rows
    normed = rms_scale(tok_ref[...], gain_ref[...]).astype(jnp.bfloat16)
    queries = mm(normed, wq_ref[...]).astype(jnp.bfloat16).astype(jnp.float32) * HD ** (-0.5)
    queries_t = queries.T.astype(jnp.bfloat16)
    qt_ref[...] = jnp.zeros_like(qt_ref)
    for h in range(heads):
        kv = h // share
        qt_ref[kv * HD : (kv + 1) * HD, h * rows : (h + 1) * rows] = queries_t[h * HD : (h + 1) * HD, :]
    keys_new = mm(normed, wk_ref[...]).astype(jnp.bfloat16)
    values_new = mm(normed, wv_ref[...]).astype(jnp.bfloat16)

    def weigh(values, weights):
        return lax.dot_general(
            values, weights, (((0,), (0,)), ((), ())), preferred_element_type=jnp.float32
        )

    scores = mm(keys_new, qt_ref[...])
    key_pos = lax.broadcasted_iota(jnp.int32, (rows, columns), 0)
    query_pos = lax.broadcasted_iota(jnp.int32, (rows, columns), 1) % rows
    scores = jnp.where(key_pos <= query_pos, scores, neg_large)
    top = jnp.max(scores, axis=0, keepdims=True)
    weights = jnp.exp(scores - top)
    top_ref[...] = top
    total_ref[...] = jnp.sum(weights, axis=0, keepdims=True)
    acc_ref[...] = weigh(values_new, weights.astype(jnp.bfloat16))

    def visit(block_idx, masked):
        start = pl.multiple_of(block_idx * key_block, key_block)
        scores = mm(kc_ref[0, pl.ds(start, key_block), :], qt_ref[...])
        if masked:
            place = start + lax.broadcasted_iota(jnp.int32, (key_block, columns), 0)
            first = length - WINDOW + 1 + lax.broadcasted_iota(jnp.int32, (1, columns), 1) % rows
            live = (place < length) & ((place < SINK) | (place >= first))
            scores = jnp.where(live, scores, neg_large)
        top_old = top_ref[...]
        top_new = jnp.maximum(top_old, jnp.max(scores, axis=0, keepdims=True))
        weights = jnp.exp(scores - top_new)
        factor = jnp.exp(top_old - top_new)
        top_ref[...] = top_new
        total_ref[...] = total_ref[...] * factor + jnp.sum(weights, axis=0, keepdims=True)
        acc_ref[...] = acc_ref[...] * factor + weigh(
            vc_ref[0, pl.ds(start, key_block), :], weights.astype(jnp.bfloat16)
        )

    blocks = (length + key_block - 1) // key_block
    low = jnp.minimum(
        (jnp.maximum(length + rows - WINDOW, 0) + key_block - 1) // key_block, blocks
    )
    high = jnp.maximum(low, length // key_block)

    def run(begin, end, masked):
        def step(block_idx, carried):
            visit(block_idx, masked)
            return carried

        lax.fori_loop(begin, end, step, 0)

    run(0, low, True)
    run(low, high, False)
    run(high, blocks, True)
    result = acc_ref[...] / total_ref[...]
    parts = []
    for h in range(heads):
        kv = h // share
        parts.append(result[kv * HD : (kv + 1) * HD, h * rows : (h + 1) * rows])
    heads_rows = jnp.concatenate(parts, axis=0).T.astype(jnp.bfloat16)
    projected = mm(heads_rows, wo_ref[...]).astype(jnp.bfloat16)
    part = rows // len(out_refs)
    for index, out_ref in enumerate(out_refs):
        out_ref[...] = projected[index * part : (index + 1) * part, :]


def attend(past_len, tokens, gain, w_query, w_key, w_value, w_out, cache_keys, cache_values):
    requests, capacity, kv_width = cache_keys.shape
    group_rows, width = tokens.shape
    rows = group_rows // requests
    key_block = math.gcd(capacity, 512)
    columns = w_query.shape[1] // HD * rows

    def whole(array):
        return pl.BlockSpec(
            array.shape, lambda i, lens: (0,) * array.ndim, pipeline_mode=pl.Buffered(1)
        )

    gain = gain.reshape(1, width)
    cache_spec = pl.BlockSpec((1, capacity, kv_width), lambda i, lens: (i, 0, 0))
    row_spec = pl.BlockSpec((rows, width), lambda i, lens: (i, 0))
    return pl.pallas_call(
        functools.partial(attend_kernel, key_block),
        out_shape=[jax.ShapeDtypeStruct((group_rows // CHUNKS, width), jnp.bfloat16)] * CHUNKS,
        grid_spec=pltpu.PrefetchScalarGridSpec(
            num_scalar_prefetch=1,
            grid=(requests,),
            in_specs=[row_spec]
            + [whole(a) for a in (gain, w_query, w_key, w_value, w_out)]
            + [cache_spec, cache_spec],
            out_specs=[pl.BlockSpec((rows // CHUNKS, width), lambda i, lens: (i, 0))] * CHUNKS,
            scratch_shapes=[
                pltpu.VMEM((kv_width, columns), jnp.bfloat16),
                pltpu.VMEM((1, columns), jnp.float32),
                pltpu.VMEM((1, columns), jnp.float32),
                pltpu.VMEM((kv_width, columns), jnp.float32),
            ],
        ),
        compiler_params=pltpu.CompilerParams(vmem_limit_bytes=48 << 20),
        cost_estimate=pl.CostEstimate(
            flops=8 * cache_keys.size * columns,
            bytes_accessed=cache_keys.size * 4,
            transcendentals=0,
        ),
        name="attend",
    )(past_len, tokens, gain, w_query, w_key, w_value, w_out, cache_keys, cache_values)


def gate_kernel(attn_ref, tok_ref, gain_ref, router_ref, chosen_ref, stream_ref, ext_ref):
    width = tok_ref.shape[1]
    stream = tok_ref[...].astype(jnp.float32) + attn_ref[...].astype(jnp.float32)
    stream_ref[...] = stream
    moe_in = rms_scale(stream, gain_ref[...]).astype(jnp.bfloat16)
    ext_ref[:, :width] = moe_in
    logits = mm(moe_in, router_ref[...])
    chosen = chosen_ref[...] > 0.0
    top = jnp.max(jnp.where(chosen, logits, neg_large), axis=-1, keepdims=True)
    weights = jnp.where(chosen, jnp.exp(jnp.where(chosen, logits, top) - top), 0.0)
    gates = weights / (0.5 * jnp.sum(weights, axis=-1, keepdims=True))
    half = gates.shape[1] // 2
    coarse = gates.astype(jnp.bfloat16).astype(jnp.float32)
    lane = lax.broadcasted_iota(jnp.int32, gates.shape, 1)
    ext_ref[:, width:] = jnp.where(lane < half, coarse, gates - coarse).astype(jnp.bfloat16)


def gate_rows(attn_rows, rows_mine, gain, router2, chosen2):
    rows, width = rows_mine.shape
    return pl.pallas_call(
        gate_kernel,
        out_shape=(
            jax.ShapeDtypeStruct((rows, width), jnp.float32),
            jax.ShapeDtypeStruct((rows, width + router2.shape[1]), jnp.bfloat16),
        ),
        name="gate_rows",
    )(attn_rows, rows_mine, gain.reshape(1, width), router2, chosen2)


def experts_kernel(
    span, me_ref, ext_ref, win_ref, wout_ref, out_ref, rank_ref, rank_t_ref, acc_ref
):
    s = pl.program_id(0)
    slots = pl.num_programs(0)
    rows, wide = ext_ref.shape
    width = acc_ref.shape[1]
    extra = wide - width
    ff_width = wout_ref.shape[1]
    first = me_ref[0] * slots

    def pick_slot(shape, dim_from, dim_to, offset):
        source = lax.broadcasted_iota(jnp.int32, shape, dim_from) % (extra // 2)
        target = lax.broadcasted_iota(jnp.int32, shape, dim_to)
        return source == target + offset

    @pl.when(s == 0)
    def _():
        choose = pick_slot((extra, 128), 0, 1, first) & (
            lax.broadcasted_iota(jnp.int32, (extra, 128), 1) < slots
        )
        choose = jnp.where(choose, 1.0, 0.0).astype(jnp.bfloat16)
        before = jnp.where(
            lax.broadcasted_iota(jnp.int32, (span, span), 1)
            < lax.broadcasted_iota(jnp.int32, (span, span), 0),
            1.0,
            0.0,
        ).astype(jnp.bfloat16)
        seen = jnp.zeros((1, 128), jnp.float32)
        for part in range(rows // span):
            here = slice(part * span, (part + 1) * span)
            used = mm(ext_ref[here, width:], choose) > 0.0
            ones = jnp.where(used, 1.0, 0.0)
            rank = mm(before, ones.astype(jnp.bfloat16)) + seen
            rank = jnp.where(used, rank, -1.0)
            seen = seen + jnp.sum(ones, axis=0, keepdims=True)
            rank_ref[here, :] = rank
            rank_t_ref[:, here] = rank.T[: rank_t_ref.shape[0], :]
        acc_ref[...] = jnp.zeros_like(acc_ref)

    rank_row = rank_t_ref[pl.ds(s, 1), :]
    count = jnp.max(rank_row).astype(jnp.int32) + 1
    chunk = math.gcd(rows, 512)
    tile_rows = 128 if rows <= MOST_ROWS else 64

    def tile(index, carried):
        base = (index * tile_rows).astype(jnp.float32)
        wanted = base + lax.broadcasted_iota(jnp.int32, (tile_rows, rows), 0).astype(jnp.float32)
        select = jnp.where(wanted == rank_row, 1.0, 0.0).astype(jnp.bfloat16)
        taken = mm(select, ext_ref[...])
        moe_in = taken[:, :width].astype(jnp.bfloat16)
        lane = lax.broadcasted_iota(jnp.int32, (tile_rows, extra), 1) % (extra // 2)
        mine = lane == first + s
        gate = jnp.sum(jnp.where(mine, taken[:, width:], 0.0), axis=1, keepdims=True)
        gate_up = mm(moe_in, win_ref[0])
        g = gate_up[:, :ff_width]
        activation = (g / (1.0 + jnp.exp(-g)) * gate_up[:, ff_width:]).astype(jnp.bfloat16)
        produced = (mm(activation, wout_ref[0]) * gate).astype(jnp.bfloat16)
        for part in range(rows // chunk):
            here = slice(part * chunk, (part + 1) * chunk)
            lane_id = lax.broadcasted_iota(jnp.int32, (chunk, 128), 1)
            column = jnp.sum(
                jnp.where(lane_id == s, rank_ref[here, :], 0.0), axis=1, keepdims=True
            )
            place = base + lax.broadcasted_iota(jnp.int32, (chunk, tile_rows), 1).astype(jnp.float32)
            spread = jnp.where(place == column, 1.0, 0.0).astype(jnp.bfloat16)
            acc_ref[here, :] = acc_ref[here, :] + mm(spread, produced)
        return carried

    lax.fori_loop(0, (count + tile_rows - 1) // tile_rows, tile, 0)

    @pl.when(s == slots - 1)
    def _():
        out_ref[...] = acc_ref[...].astype(jnp.bfloat16)


def run_experts(me, gathered, expert_in, expert_out):
    rows, wide = gathered.shape
    span = math.gcd(rows, 256)
    slots, width, double = expert_in.shape
    ff_width = expert_out.shape[1]
    return pl.pallas_call(
        functools.partial(experts_kernel, span),
        out_shape=jax.ShapeDtypeStruct((rows, width), jnp.bfloat16),
        grid_spec=pltpu.PrefetchScalarGridSpec(
            num_scalar_prefetch=1,
            grid=(slots,),
            in_specs=[
                pl.BlockSpec((rows, wide), lambda i, me: (0, 0), pipeline_mode=pl.Buffered(1)),
                pl.BlockSpec((1, width, double), lambda i, me: (i, 0, 0)),
                pl.BlockSpec((1, ff_width, width), lambda i, me: (i, 0, 0)),
            ],
            out_specs=pl.BlockSpec((rows, width), lambda i, me: (0, 0), pipeline_mode=pl.Buffered(1)),
            scratch_shapes=[
                pltpu.VMEM((rows, 128), jnp.float32),
                pltpu.VMEM((-(-slots // 8) * 8, rows), jnp.float32),
                pltpu.VMEM((rows, width), jnp.float32),
            ],
        ),
        compiler_params=pltpu.CompilerParams(vmem_limit_bytes=64000 << 10),
        cost_estimate=pl.CostEstimate(
            flops=16 * rows * width * ff_width * 8,
            bytes_accessed=expert_in.size * 2 + expert_out.size * 2 + rows * (wide + width) * 2,
            transcendentals=0,
        ),
        name="run_experts",
    )(me, gathered, expert_in, expert_out)


def finish_kernel(*refs):
    gain_ref, out_ref = refs[-2:]
    part = refs[0].shape[0]
    for index in range(CHUNKS):
        combined = refs[index][...] + refs[CHUNKS + index][...].astype(jnp.float32)
        out_ref[index * part : (index + 1) * part, :] = rms_scale(combined, gain_ref[...]).astype(
            jnp.bfloat16
        )


def finish(streams, mixes, gain):
    part, width = streams[0].shape
    return pl.pallas_call(
        finish_kernel,
        out_shape=jax.ShapeDtypeStruct((part * CHUNKS, width), jnp.bfloat16),
        name="finish",
    )(*streams, *mixes, gain.reshape(1, width))


def choose_slots(slot_owner, routes, split_pick):
    slot_ids = jnp.arange(slot_owner.shape[0], dtype=jnp.int32)
    same_owner = slot_owner[:, None] == slot_owner[None, :]
    slot_rank = jnp.sum(
        (same_owner & (slot_ids[None, :] < slot_ids[:, None])).astype(jnp.int32), axis=1
    )
    replicas = jnp.sum(same_owner.astype(jnp.int32), axis=1)
    hits = (slot_owner[None, None, :] == routes[:, :, None]) & (
        slot_rank[None, None, :] == split_pick[:, :, None] % replicas[None, None, :]
    )
    return jnp.any(hits, axis=1).astype(jnp.float32)


def shards(
    tokens,
    past_len,
    cache_keys,
    cache_values,
    attn_gain,
    w_query,
    w_key,
    w_value,
    w_out,
    moe_gain,
    router,
    expert_in,
    expert_out,
    final_gain,
    slot_owner,
    routes,
    split_pick,
):
    chosen = choose_slots(slot_owner, routes, split_pick)
    chosen2 = jnp.concatenate([chosen, chosen], axis=1)
    owner2 = jnp.concatenate([slot_owner, slot_owner])
    pick = owner2[None, :] == jnp.arange(router.shape[1], dtype=jnp.int32)[:, None]
    router2 = mm(router, pick.astype(jnp.bfloat16)).astype(jnp.bfloat16)
    projected = attend(
        past_len, tokens, attn_gain, w_query, w_key, w_value, w_out, cache_keys, cache_values
    )
    tok_dev = tokens.shape[0] // lax.axis_size("dp")
    part = tok_dev // CHUNKS
    me = lax.axis_index("expert").astype(jnp.int32).reshape(1)
    streams, mixes = [], []
    for index in range(CHUNKS):
        attn_rows = lax.psum_scatter(projected[index], "dp", scatter_dimension=0, tiled=True)
        begin = lax.axis_index("dp") * tok_dev + index * part
        rows_mine = lax.dynamic_slice_in_dim(tokens, begin, part, 0)
        here = slice(index * part, (index + 1) * part)
        stream, extended = gate_rows(attn_rows, rows_mine, moe_gain, router2, chosen2[here])
        gathered = lax.all_gather(extended, "expert", axis=0, tiled=True)
        partial = run_experts(me, gathered, expert_in, expert_out)
        mixed = lax.psum_scatter(partial, "expert", scatter_dimension=0, tiled=True)
        streams.append(stream)
        mixes.append(mixed)
    return finish(streams, mixes, final_gain)


def solution(mesh):
    return jax.shard_map(
        shards,
        mesh=mesh,
        in_specs=(
            P("expert", None),
            P("expert"),
            P("expert", None, "dp"),
            P("expert", None, "dp"),
            P(),
            P(None, "dp"),
            P(None, "dp"),
            P(None, "dp"),
            P("dp", None),
            P(),
            P(),
            P("expert", None, None),
            P("expert", None, None),
            P(),
            P(),
            P(("expert", "dp"), None),
            P(("expert", "dp"), None),
        ),
        out_specs=P(("expert", "dp"), None),
        check_vma=False,
    )
```

```python
import functools
import math

import jax
import jax.numpy as jnp
from jax import lax
from jax.experimental import pallas as pl
from jax.experimental.pallas import tpu as pltpu
from jax.sharding import PartitionSpec as P

HD = 64
SINK = 4
WINDOW = 4096
MOST_ROWS = 2048

epsilon = 1e-05
neg_large = -1e30


def rms_scale(values, gain):
    widened = values.astype(jnp.float32)
    mean_square = jnp.mean(widened * widened, axis=-1, keepdims=True)
    return widened * lax.rsqrt(mean_square + epsilon) * gain


def mm(a, b):
    return jnp.dot(a, b, preferred_element_type=jnp.float32)


def attend_kernel(
    key_block, len_ref, tok_ref, gain_ref, wq_ref, wk_ref, wv_ref, wo_ref, kc_ref, vc_ref,
    out_ref, qt_ref, top_ref, total_ref, acc_ref,
):
    length = len_ref[pl.program_id(0)]
    rows = tok_ref.shape[0]
    heads = wq_ref.shape[1] // HD
    kv_local = wk_ref.shape[1] // HD
    share = heads // kv_local
    columns = heads * rows
    normed = rms_scale(tok_ref[...], gain_ref[...]).astype(jnp.bfloat16)
    queries = mm(normed, wq_ref[...]).astype(jnp.bfloat16).astype(jnp.float32) * HD ** (-0.5)
    queries_t = queries.T.astype(jnp.bfloat16)
    qt_ref[...] = jnp.zeros_like(qt_ref)
    for h in range(heads):
        kv = h // share
        qt_ref[kv * HD : (kv + 1) * HD, h * rows : (h + 1) * rows] = queries_t[h * HD : (h + 1) * HD, :]
    keys_new = mm(normed, wk_ref[...]).astype(jnp.bfloat16)
    values_new = mm(normed, wv_ref[...]).astype(jnp.bfloat16)

    def weigh(values, weights):
        return lax.dot_general(
            values, weights, (((0,), (0,)), ((), ())), preferred_element_type=jnp.float32
        )

    scores = mm(keys_new, qt_ref[...])
    key_pos = lax.broadcasted_iota(jnp.int32, (rows, columns), 0)
    query_pos = lax.broadcasted_iota(jnp.int32, (rows, columns), 1) % rows
    scores = jnp.where(key_pos <= query_pos, scores, neg_large)
    top = jnp.max(scores, axis=0, keepdims=True)
    weights = jnp.exp(scores - top)
    top_ref[...] = top
    total_ref[...] = jnp.sum(weights, axis=0, keepdims=True)
    acc_ref[...] = weigh(values_new, weights.astype(jnp.bfloat16))

    def visit(block_idx, masked):
        start = pl.multiple_of(block_idx * key_block, key_block)
        scores = mm(kc_ref[0, pl.ds(start, key_block), :], qt_ref[...])
        if masked:
            place = start + lax.broadcasted_iota(jnp.int32, (key_block, columns), 0)
            first = length - WINDOW + 1 + lax.broadcasted_iota(jnp.int32, (1, columns), 1) % rows
            live = (place < length) & ((place < SINK) | (place >= first))
            scores = jnp.where(live, scores, neg_large)
        top_old = top_ref[...]
        top_new = jnp.maximum(top_old, jnp.max(scores, axis=0, keepdims=True))
        weights = jnp.exp(scores - top_new)
        factor = jnp.exp(top_old - top_new)
        top_ref[...] = top_new
        total_ref[...] = total_ref[...] * factor + jnp.sum(weights, axis=0, keepdims=True)
        acc_ref[...] = acc_ref[...] * factor + weigh(
            vc_ref[0, pl.ds(start, key_block), :], weights.astype(jnp.bfloat16)
        )

    blocks = (length + key_block - 1) // key_block
    low = jnp.minimum(
        (jnp.maximum(length + rows - WINDOW, 0) + key_block - 1) // key_block, blocks
    )
    high = jnp.maximum(low, length // key_block)

    def run(begin, end, masked):
        def step(block_idx, carried):
            visit(block_idx, masked)
            return carried

        lax.fori_loop(begin, end, step, 0)

    run(0, low, True)
    run(low, high, False)
    run(high, blocks, True)
    result = acc_ref[...] / total_ref[...]
    parts = []
    for h in range(heads):
        kv = h // share
        parts.append(result[kv * HD : (kv + 1) * HD, h * rows : (h + 1) * rows])
    heads_rows = jnp.concatenate(parts, axis=0).T.astype(jnp.bfloat16)
    out_ref[...] = mm(heads_rows, wo_ref[...]).astype(jnp.bfloat16)


def attend(past_len, tokens, gain, w_query, w_key, w_value, w_out, cache_keys, cache_values):
    requests, capacity, kv_width = cache_keys.shape
    group_rows, width = tokens.shape
    rows = group_rows // requests
    key_block = math.gcd(capacity, 512)
    columns = w_query.shape[1] // HD * rows

    def whole(array):
        return pl.BlockSpec(
            array.shape, lambda i, lens: (0,) * array.ndim, pipeline_mode=pl.Buffered(1)
        )

    gain = gain.reshape(1, width)
    cache_spec = pl.BlockSpec((1, capacity, kv_width), lambda i, lens: (i, 0, 0))
    row_spec = pl.BlockSpec((rows, width), lambda i, lens: (i, 0))
    return pl.pallas_call(
        functools.partial(attend_kernel, key_block),
        out_shape=jax.ShapeDtypeStruct((group_rows, width), jnp.bfloat16),
        grid_spec=pltpu.PrefetchScalarGridSpec(
            num_scalar_prefetch=1,
            grid=(requests,),
            in_specs=[row_spec]
            + [whole(a) for a in (gain, w_query, w_key, w_value, w_out)]
            + [cache_spec, cache_spec],
            out_specs=row_spec,
            scratch_shapes=[
                pltpu.VMEM((kv_width, columns), jnp.bfloat16),
                pltpu.VMEM((1, columns), jnp.float32),
                pltpu.VMEM((1, columns), jnp.float32),
                pltpu.VMEM((kv_width, columns), jnp.float32),
            ],
        ),
        compiler_params=pltpu.CompilerParams(vmem_limit_bytes=48 << 20),
        name="attend",
    )(past_len, tokens, gain, w_query, w_key, w_value, w_out, cache_keys, cache_values)


def start_if(cond, copy):
    pl.when(cond)(copy.start)


def greet(targets):
    barrier = pltpu.get_barrier_semaphore()
    total = 0
    for cond, device in targets:

        @pl.when(cond)
        def _():
            pl.semaphore_signal(
                barrier, inc=1, device_id=device, device_id_type=pl.DeviceIdType.MESH
            )

        total = total + jnp.where(cond, 1, 0)
    pl.semaphore_wait(barrier, total)


def send(src, dst, send_sem, recv_sem, device):
    return pltpu.make_async_remote_copy(
        src_ref=src,
        dst_ref=dst,
        send_sem=send_sem,
        recv_sem=recv_sem,
        device_id=device,
        device_id_type=pl.DeviceIdType.MESH,
    )


def exchange_kernel(
    dp_size, chips, proj_ref, tok_ref, gain_ref, router_ref, chosen_ref,
    stream_ref, all_ref,
    mine_ref, got_ref, ext_ref,
    tok_sem, own_sem, rs_send, rs_recv, up_send, up_recv, dn_send, dn_recv, sib_send, sib_recv,
):
    rows, wide = ext_ref.shape
    width = mine_ref.shape[1]
    dp, ex = lax.axis_index("dp"), lax.axis_index("expert")
    chip, core = ex // 2, ex % 2
    upper, lower = chip < chips - 1, chip > 0
    true = chip >= 0
    sibling = (dp, chip * 2 + 1 - core)
    above = (dp, jnp.minimum(chip + 1, chips - 1) * 2 + core)
    below = (dp, jnp.maximum(chip - 1, 0) * 2 + core)
    load = pltpu.make_async_copy(tok_ref.at[pl.ds(dp * rows, rows)], mine_ref, tok_sem)
    load.start()
    greet(
        [(true, (lax.rem(dp + k, dp_size), ex)) for k in range(1, dp_size)]
        + [(true, sibling), (upper, above), (lower, below)]
    )
    copies = []
    for k in range(1, dp_size):
        peer = lax.rem(dp + k, dp_size)
        copy = send(
            proj_ref.at[pl.ds(peer * rows, rows)],
            got_ref.at[k - 1],
            rs_send.at[k - 1],
            rs_recv.at[k - 1],
            (peer, ex),
        )
        copy.start()
        copies.append(copy)
    load.wait()
    attn = proj_ref[pl.ds(dp * rows, rows), :].astype(jnp.float32)
    for k, copy in enumerate(copies):
        copy.wait()
        attn = attn + got_ref[k].astype(jnp.float32)
    stream = mine_ref[...].astype(jnp.float32) + attn
    stream_ref[...] = stream
    moe_in = rms_scale(stream, gain_ref[...]).astype(jnp.bfloat16)
    ext_ref[:, :width] = moe_in
    logits = mm(moe_in, router_ref[...])
    chosen = chosen_ref[...] > 0.0
    top = jnp.max(jnp.where(chosen, logits, neg_large), axis=-1, keepdims=True)
    weights = jnp.where(chosen, jnp.exp(jnp.where(chosen, logits, top) - top), 0.0)
    gates = weights / (0.5 * jnp.sum(weights, axis=-1, keepdims=True))
    half = gates.shape[1] // 2
    coarse = gates.astype(jnp.bfloat16).astype(jnp.float32)
    lane = lax.broadcasted_iota(jnp.int32, gates.shape, 1)
    ext_ref[:, width:] = jnp.where(lane < half, coarse, gates - coarse).astype(jnp.bfloat16)

    def block(chip_id, core_id):
        bounded = jnp.clip(chip_id, 0, chips - 1)
        return all_ref.at[pl.ds((bounded * 2 + core_id) * rows, rows)]

    own = pltpu.make_async_copy(ext_ref, block(chip, core), own_sem)
    own.start()

    def hop(chip_id, src, sends, recvs, index, target):
        return send(src, block(chip_id, core), sends.at[index], recvs.at[index], target)

    waits = []
    for s in range(chips):
        if s < chips - 1:
            for sign, edge, target, sends, recvs in (
                (-1, upper, above, up_send, up_recv),
                (1, lower, below, dn_send, dn_recv),
            ):
                origin = chip + sign * s
                cond = edge & (origin >= 0) & (origin < chips)
                copy = hop(origin, ext_ref if s == 0 else block(origin, core), sends, recvs, s, target)
                start_if(cond, copy)
                waits.append((cond, copy))
        for sign, index in ((-1, s), (1, chips - 1 + s)):
            origin = chip + sign * s
            if s == 0 and sign == 1:
                continue
            cond = (origin >= 0) & (origin < chips)
            copy = hop(origin, ext_ref if s == 0 else block(origin, core), sib_send, sib_recv, index, sibling)
            start_if(cond, copy)
            waits.append((cond, copy))
        if s < chips - 1:
            for sign, target, sends, recvs in (
                (-1, above, up_send, up_recv),
                (1, below, dn_send, dn_recv),
            ):
                origin = chip + sign * (s + 1)
                cond = (origin >= 0) & (origin < chips)
                copy = hop(origin, ext_ref, sends, recvs, s, target)
                pl.when(cond)(copy.wait_recv)
    for cond, copy in waits:
        pl.when(cond)(copy.wait_send)
    for s in range(chips):
        for sign, index in ((-1, s), (1, chips - 1 + s)):
            if s == 0 and sign == 1:
                continue
            origin = chip + sign * s
            copy = send(ext_ref, block(origin, 1 - core), sib_send.at[index], sib_recv.at[index], sibling)
            pl.when((origin >= 0) & (origin < chips))(copy.wait_recv)
    own.wait()


def exchange(projected, tokens, gain, router2, chosen2, dp_size, ex_size):
    group_rows, width = tokens.shape
    rows = group_rows // dp_size
    wide = width + router2.shape[1]
    chips = ex_size // 2
    dma = pltpu.SemaphoreType.DMA
    vmem = pl.BlockSpec(memory_space=pltpu.VMEM)
    hbm = pl.BlockSpec(memory_space=pl.ANY)
    return pl.pallas_call(
        functools.partial(exchange_kernel, dp_size, chips),
        out_shape=(
            jax.ShapeDtypeStruct((rows, width), jnp.float32),
            jax.ShapeDtypeStruct((ex_size * rows, wide), jnp.bfloat16),
        ),
        in_specs=[vmem, hbm, vmem, vmem, vmem],
        out_specs=(vmem, hbm),
        scratch_shapes=[
            pltpu.VMEM((rows, width), jnp.bfloat16),
            pltpu.VMEM((dp_size - 1, rows, width), jnp.bfloat16),
            pltpu.VMEM((rows, wide), jnp.bfloat16),
            dma,
            dma,
            dma((dp_size - 1,)),
            dma((dp_size - 1,)),
        ]
        + [dma((chips - 1,))] * 4
        + [dma((2 * chips - 1,))] * 2,
        compiler_params=pltpu.CompilerParams(
            collective_id=0, has_side_effects=True, vmem_limit_bytes=40 << 20
        ),
        name="exchange",
    )(projected, tokens, gain.reshape(1, width), router2, chosen2)


def collect_kernel(
    chips, part_ref, stream_ref, gain_ref, out_ref,
    sib_ref, sum_ref, up_ref, dn_ref,
    sib_send, sib_recv, up_send, up_recv, dn_send, dn_recv,
):
    rows = stream_ref.shape[0]
    dp, ex = lax.axis_index("dp"), lax.axis_index("expert")
    chip, core = ex // 2, ex % 2
    upper, lower = chip < chips - 1, chip > 0
    sibling = (dp, chip * 2 + 1 - core)
    above = (dp, jnp.minimum(chip + 1, chips - 1) * 2 + core)
    below = (dp, jnp.maximum(chip - 1, 0) * 2 + core)
    greet([(chip >= 0, sibling), (upper, above), (lower, below)])
    order = [k for pair in zip(range(chips), reversed(range(chips))) for k in pair][:chips]
    swaps = []
    for d in order:
        copy = send(
            part_ref.at[pl.ds((d * 2 + 1 - core) * rows, rows)],
            sib_ref.at[d],
            sib_send.at[d],
            sib_recv.at[d],
            sibling,
        )
        copy.start()
        swaps.append(copy)
    for d, copy in zip(order, swaps):
        copy.wait_recv()
        mine = part_ref[pl.ds((d * 2 + core) * rows, rows), :].astype(jnp.float32)
        sum_ref[d] = (mine + sib_ref[d].astype(jnp.float32)).astype(jnp.bfloat16)

    waits = []
    for s in range(1, chips):
        for index, (edge, target, buf, sends, recvs) in enumerate(
            ((lower, below, dn_ref, dn_send, dn_recv), (upper, above, up_ref, up_send, up_recv))
        ):
            place = chips - 1 - chip if index == 0 else chip
            hop = s - 1 - place
            dest = hop if index == 0 else chips - 1 - hop
            bounded = jnp.clip(dest, 0, chips - 1)
            valid = edge & (hop >= 0) & ((dest < chip) if index == 0 else (dest > chip))
            copy = send(
                sum_ref.at[bounded], buf.at[s - 1], sends.at[s - 1], recvs.at[s - 1], target
            )
            if s > 1:

                @pl.when(valid & (place > 0))
                def _():
                    total = sum_ref[bounded].astype(jnp.float32)
                    total = total + buf[s - 2].astype(jnp.float32)
                    sum_ref[bounded] = total.astype(jnp.bfloat16)

            start_if(valid, copy)
            waits.append((valid, copy))
        for index, (edge, target, buf, sends, recvs) in enumerate(
            ((upper, below, dn_ref, dn_send, dn_recv), (lower, above, up_ref, up_send, up_recv))
        ):
            place = chips - 1 - chip if index == 0 else chip
            hop = s - place
            dest = hop if index == 0 else chips - 1 - hop
            valid = edge & (hop >= 0) & ((dest <= chip) if index == 0 else (dest >= chip))
            copy = send(sum_ref.at[0], buf.at[s - 1], sends.at[s - 1], recvs.at[s - 1], target)
            pl.when(valid)(copy.wait_recv)
    last = chips - 2
    total = stream_ref[...] + sum_ref[chip].astype(jnp.float32)
    total = total + jnp.where(upper, dn_ref[last].astype(jnp.float32), 0.0)
    total = total + jnp.where(lower, up_ref[last].astype(jnp.float32), 0.0)
    out_ref[...] = rms_scale(total, gain_ref[...]).astype(jnp.bfloat16)
    for cond, copy in waits:
        pl.when(cond)(copy.wait_send)
    for copy in swaps:
        copy.wait_send()


def collect(partial, stream, gain, ex_size):
    rows, width = stream.shape
    chips = ex_size // 2
    dma = pltpu.SemaphoreType.DMA
    vmem = pl.BlockSpec(memory_space=pltpu.VMEM)
    blocks = pltpu.VMEM((chips, rows, width), jnp.bfloat16)
    landing = pltpu.VMEM((chips - 1, rows, width), jnp.bfloat16)
    return pl.pallas_call(
        functools.partial(collect_kernel, chips),
        out_shape=jax.ShapeDtypeStruct((rows, width), jnp.bfloat16),
        in_specs=[vmem] * 3,
        out_specs=vmem,
        scratch_shapes=[blocks, blocks, landing, landing, dma((chips,)), dma((chips,))]
        + [dma((chips - 1,))] * 4,
        compiler_params=pltpu.CompilerParams(
            collective_id=1, has_side_effects=True, vmem_limit_bytes=56 << 20
        ),
        name="collect",
    )(partial, stream, gain.reshape(1, width))


def experts_kernel(
    span, me_ref, ext_ref, win_ref, wout_ref, out_ref, rank_ref, rank_t_ref, acc_ref
):
    s = pl.program_id(0)
    slots = pl.num_programs(0)
    rows, wide = ext_ref.shape
    width = acc_ref.shape[1]
    extra = wide - width
    ff_width = wout_ref.shape[1]
    first = me_ref[0] * slots

    def pick_slot(shape, dim_from, dim_to, offset):
        source = lax.broadcasted_iota(jnp.int32, shape, dim_from) % (extra // 2)
        target = lax.broadcasted_iota(jnp.int32, shape, dim_to)
        return source == target + offset

    @pl.when(s == 0)
    def _():
        choose = pick_slot((extra, 128), 0, 1, first) & (
            lax.broadcasted_iota(jnp.int32, (extra, 128), 1) < slots
        )
        choose = jnp.where(choose, 1.0, 0.0).astype(jnp.bfloat16)
        before = jnp.where(
            lax.broadcasted_iota(jnp.int32, (span, span), 1)
            < lax.broadcasted_iota(jnp.int32, (span, span), 0),
            1.0,
            0.0,
        ).astype(jnp.bfloat16)
        seen = jnp.zeros((1, 128), jnp.float32)
        for part in range(rows // span):
            here = slice(part * span, (part + 1) * span)
            used = mm(ext_ref[here, width:], choose) > 0.0
            ones = jnp.where(used, 1.0, 0.0)
            rank = mm(before, ones.astype(jnp.bfloat16)) + seen
            rank = jnp.where(used, rank, -1.0)
            seen = seen + jnp.sum(ones, axis=0, keepdims=True)
            rank_ref[here, :] = rank
            rank_t_ref[:, here] = rank.T[: rank_t_ref.shape[0], :]
        acc_ref[...] = jnp.zeros_like(acc_ref)

    rank_row = rank_t_ref[pl.ds(s, 1), :]
    count = jnp.max(rank_row).astype(jnp.int32) + 1
    chunk = math.gcd(rows, 512)
    tile_rows = 256 if rows <= MOST_ROWS else 64

    def tile(index, carried):
        base = (index * tile_rows).astype(jnp.float32)
        wanted = base + lax.broadcasted_iota(jnp.int32, (tile_rows, rows), 0).astype(jnp.float32)
        select = jnp.where(wanted == rank_row, 1.0, 0.0).astype(jnp.bfloat16)
        taken = mm(select, ext_ref[...])
        moe_in = taken[:, :width].astype(jnp.bfloat16)
        lane = lax.broadcasted_iota(jnp.int32, (tile_rows, extra), 1) % (extra // 2)
        mine = lane == first + s
        gate = jnp.sum(jnp.where(mine, taken[:, width:], 0.0), axis=1, keepdims=True)
        gate_up = mm(moe_in, win_ref[0])
        g = gate_up[:, :ff_width]
        activation = (g / (1.0 + jnp.exp(-g)) * gate_up[:, ff_width:]).astype(jnp.bfloat16)
        produced = (mm(activation, wout_ref[0]) * gate).astype(jnp.bfloat16)
        for part in range(rows // chunk):
            here = slice(part * chunk, (part + 1) * chunk)
            lane_id = lax.broadcasted_iota(jnp.int32, (chunk, 128), 1)
            column = jnp.sum(
                jnp.where(lane_id == s, rank_ref[here, :], 0.0), axis=1, keepdims=True
            )
            place = base + lax.broadcasted_iota(jnp.int32, (chunk, tile_rows), 1).astype(jnp.float32)
            spread = jnp.where(place == column, 1.0, 0.0).astype(jnp.bfloat16)
            acc_ref[here, :] = acc_ref[here, :] + mm(spread, produced)
        return carried

    lax.fori_loop(0, (count + tile_rows - 1) // tile_rows, tile, 0)

    @pl.when(s == slots - 1)
    def _():
        out_ref[...] = acc_ref[...].astype(jnp.bfloat16)


def run_experts(me, gathered, expert_in, expert_out, span):
    rows, wide = gathered.shape
    slots, width, double = expert_in.shape
    ff_width = expert_out.shape[1]
    return pl.pallas_call(
        functools.partial(experts_kernel, span),
        out_shape=jax.ShapeDtypeStruct((rows, width), jnp.bfloat16),
        grid_spec=pltpu.PrefetchScalarGridSpec(
            num_scalar_prefetch=1,
            grid=(slots,),
            in_specs=[
                pl.BlockSpec((rows, wide), lambda i, me: (0, 0), pipeline_mode=pl.Buffered(1)),
                pl.BlockSpec((1, width, double), lambda i, me: (i, 0, 0)),
                pl.BlockSpec((1, ff_width, width), lambda i, me: (i, 0, 0)),
            ],
            out_specs=pl.BlockSpec((rows, width), lambda i, me: (0, 0), pipeline_mode=pl.Buffered(1)),
            scratch_shapes=[
                pltpu.VMEM((rows, 128), jnp.float32),
                pltpu.VMEM((-(-slots // 8) * 8, rows), jnp.float32),
                pltpu.VMEM((rows, width), jnp.float32),
            ],
        ),
        compiler_params=pltpu.CompilerParams(vmem_limit_bytes=64000 << 10),
        name="run_experts",
    )(me, gathered, expert_in, expert_out)


def choose_slots(slot_owner, routes, split_pick):
    slot_ids = jnp.arange(slot_owner.shape[0], dtype=jnp.int32)
    same_owner = slot_owner[:, None] == slot_owner[None, :]
    slot_rank = jnp.sum(
        (same_owner & (slot_ids[None, :] < slot_ids[:, None])).astype(jnp.int32), axis=1
    )
    replicas = jnp.sum(same_owner.astype(jnp.int32), axis=1)
    hits = (slot_owner[None, None, :] == routes[:, :, None]) & (
        slot_rank[None, None, :] == split_pick[:, :, None] % replicas[None, None, :]
    )
    return jnp.any(hits, axis=1).astype(jnp.float32)


def shards(
    tokens,
    past_len,
    cache_keys,
    cache_values,
    attn_gain,
    w_query,
    w_key,
    w_value,
    w_out,
    moe_gain,
    router,
    expert_in,
    expert_out,
    final_gain,
    slot_owner,
    routes,
    split_pick,
):
    chosen = choose_slots(slot_owner, routes, split_pick)
    chosen2 = jnp.concatenate([chosen, chosen], axis=1)
    owner2 = jnp.concatenate([slot_owner, slot_owner])
    pick = owner2[None, :] == jnp.arange(router.shape[1], dtype=jnp.int32)[:, None]
    router2 = mm(router, pick.astype(jnp.bfloat16)).astype(jnp.bfloat16)
    projected = attend(
        past_len, tokens, attn_gain, w_query, w_key, w_value, w_out, cache_keys, cache_values
    )
    dp_size, ex_size = lax.axis_size("dp"), lax.axis_size("expert")
    tok_dev = tokens.shape[0] // dp_size
    stream, gathered = exchange(
        projected, tokens, moe_gain, router2, chosen2, dp_size, ex_size
    )
    me = lax.axis_index("expert").astype(jnp.int32).reshape(1)
    partial = run_experts(me, gathered, expert_in, expert_out, tok_dev)
    return collect(partial, stream, final_gain, ex_size)


def solution(mesh):
    return jax.shard_map(
        shards,
        mesh=mesh,
        in_specs=(
            P("expert", None),
            P("expert"),
            P("expert", None, "dp"),
            P("expert", None, "dp"),
            P(),
            P(None, "dp"),
            P(None, "dp"),
            P(None, "dp"),
            P("dp", None),
            P(),
            P(),
            P("expert", None, None),
            P("expert", None, None),
            P(),
            P(),
            P(("expert", "dp"), None),
            P(("expert", "dp"), None),
        ),
        out_specs=P(("expert", "dp"), None),
        check_vma=False,
    )
```

```python
import functools
import math

import jax
import jax.numpy as jnp
from jax import lax
from jax.experimental import pallas as pl
from jax.experimental.pallas import tpu as pltpu
from jax.sharding import PartitionSpec as P

HD = 64
SINK = 4
WINDOW = 4096
MOST_ROWS = 2048

epsilon = 1e-05
neg_large = -1e30


def rms_scale(values, gain):
    widened = values.astype(jnp.float32)
    mean_square = jnp.mean(widened * widened, axis=-1, keepdims=True)
    return widened * lax.rsqrt(mean_square + epsilon) * gain


def mm(a, b):
    return jnp.dot(a, b, preferred_element_type=jnp.float32)


def attend_kernel(
    key_block, len_ref, tok_ref, gain_ref, wq_ref, wk_ref, wv_ref, wo_ref, kc_ref, vc_ref,
    out_ref, qt_ref, top_ref, total_ref, acc_ref,
):
    length = len_ref[pl.program_id(0)]
    rows = tok_ref.shape[0]
    heads = wq_ref.shape[1] // HD
    kv_local = wk_ref.shape[1] // HD
    share = heads // kv_local
    columns = heads * rows
    normed = rms_scale(tok_ref[...], gain_ref[...]).astype(jnp.bfloat16)
    queries = mm(normed, wq_ref[...]).astype(jnp.bfloat16).astype(jnp.float32) * HD ** (-0.5)
    queries_t = queries.T.astype(jnp.bfloat16)
    qt_ref[...] = jnp.zeros_like(qt_ref)
    for h in range(heads):
        kv = h // share
        qt_ref[kv * HD : (kv + 1) * HD, h * rows : (h + 1) * rows] = queries_t[h * HD : (h + 1) * HD, :]
    keys_new = mm(normed, wk_ref[...]).astype(jnp.bfloat16)
    values_new = mm(normed, wv_ref[...]).astype(jnp.bfloat16)

    def weigh(values, weights):
        return lax.dot_general(
            values, weights, (((0,), (0,)), ((), ())), preferred_element_type=jnp.float32
        )

    scores = mm(keys_new, qt_ref[...])
    key_pos = lax.broadcasted_iota(jnp.int32, (rows, columns), 0)
    query_pos = lax.broadcasted_iota(jnp.int32, (rows, columns), 1) % rows
    scores = jnp.where(key_pos <= query_pos, scores, neg_large)
    top = jnp.max(scores, axis=0, keepdims=True)
    weights = jnp.exp(scores - top)
    top_ref[...] = top
    total_ref[...] = jnp.sum(weights, axis=0, keepdims=True)
    acc_ref[...] = weigh(values_new, weights.astype(jnp.bfloat16))

    def visit(block_idx, masked):
        start = pl.multiple_of(block_idx * key_block, key_block)
        scores = mm(kc_ref[0, pl.ds(start, key_block), :], qt_ref[...])
        if masked:
            place = start + lax.broadcasted_iota(jnp.int32, (key_block, columns), 0)
            first = length - WINDOW + 1 + lax.broadcasted_iota(jnp.int32, (1, columns), 1) % rows
            live = (place < length) & ((place < SINK) | (place >= first))
            scores = jnp.where(live, scores, neg_large)
        top_old = top_ref[...]
        top_new = jnp.maximum(top_old, jnp.max(scores, axis=0, keepdims=True))
        weights = jnp.exp(scores - top_new)
        factor = jnp.exp(top_old - top_new)
        top_ref[...] = top_new
        total_ref[...] = total_ref[...] * factor + jnp.sum(weights, axis=0, keepdims=True)
        acc_ref[...] = acc_ref[...] * factor + weigh(
            vc_ref[0, pl.ds(start, key_block), :], weights.astype(jnp.bfloat16)
        )

    blocks = (length + key_block - 1) // key_block
    low = jnp.minimum(
        (jnp.maximum(length + rows - WINDOW, 0) + key_block - 1) // key_block, blocks
    )
    high = jnp.maximum(low, length // key_block)

    def run(begin, end, masked):
        def step(block_idx, carried):
            visit(block_idx, masked)
            return carried

        lax.fori_loop(begin, end, step, 0)

    run(0, low, True)
    run(low, high, False)
    run(high, blocks, True)
    result = acc_ref[...] / total_ref[...]
    parts = []
    for h in range(heads):
        kv = h // share
        parts.append(result[kv * HD : (kv + 1) * HD, h * rows : (h + 1) * rows])
    heads_rows = jnp.concatenate(parts, axis=0).T.astype(jnp.bfloat16)
    out_ref[...] = mm(heads_rows, wo_ref[...]).astype(jnp.bfloat16)


def attend(past_len, tokens, gain, w_query, w_key, w_value, w_out, cache_keys, cache_values):
    requests, capacity, kv_width = cache_keys.shape
    group_rows, width = tokens.shape
    rows = group_rows // requests
    key_block = math.gcd(capacity, 512)
    columns = w_query.shape[1] // HD * rows

    def whole(array):
        return pl.BlockSpec(
            array.shape, lambda i, lens: (0,) * array.ndim, pipeline_mode=pl.Buffered(1)
        )

    gain = gain.reshape(1, width)
    cache_spec = pl.BlockSpec((1, capacity, kv_width), lambda i, lens: (i, 0, 0))
    row_spec = pl.BlockSpec((rows, width), lambda i, lens: (i, 0))
    return pl.pallas_call(
        functools.partial(attend_kernel, key_block),
        out_shape=jax.ShapeDtypeStruct((group_rows, width), jnp.bfloat16),
        grid_spec=pltpu.PrefetchScalarGridSpec(
            num_scalar_prefetch=1,
            grid=(requests,),
            in_specs=[row_spec]
            + [whole(a) for a in (gain, w_query, w_key, w_value, w_out)]
            + [cache_spec, cache_spec],
            out_specs=row_spec,
            scratch_shapes=[
                pltpu.VMEM((kv_width, columns), jnp.bfloat16),
                pltpu.VMEM((1, columns), jnp.float32),
                pltpu.VMEM((1, columns), jnp.float32),
                pltpu.VMEM((kv_width, columns), jnp.float32),
            ],
        ),
        compiler_params=pltpu.CompilerParams(vmem_limit_bytes=48 << 20),
        name="attend",
    )(past_len, tokens, gain, w_query, w_key, w_value, w_out, cache_keys, cache_values)


def start_if(cond, copy):
    pl.when(cond)(copy.start)


def greet(targets):
    barrier = pltpu.get_barrier_semaphore()
    total = 0
    for cond, device in targets:

        @pl.when(cond)
        def _():
            pl.semaphore_signal(
                barrier, inc=1, device_id=device, device_id_type=pl.DeviceIdType.MESH
            )

        total = total + jnp.where(cond, 1, 0)
    pl.semaphore_wait(barrier, total)


def send(src, dst, send_sem, recv_sem, device):
    return pltpu.make_async_remote_copy(
        src_ref=src,
        dst_ref=dst,
        send_sem=send_sem,
        recv_sem=recv_sem,
        device_id=device,
        device_id_type=pl.DeviceIdType.MESH,
    )


def exchange_kernel(
    dp_size, chips, proj_ref, tok_ref, gain_ref, router_ref, chosen_ref,
    stream_ref, all_ref,
    mine_ref, got_ref, ext_ref,
    tok_sem, own_sem, rs_send, rs_recv, up_send, up_recv, dn_send, dn_recv, sib_send, sib_recv,
):
    rows, wide = ext_ref.shape
    width = mine_ref.shape[1]
    dp, ex = lax.axis_index("dp"), lax.axis_index("expert")
    chip, core = ex // 2, ex % 2
    upper, lower = chip < chips - 1, chip > 0
    true = chip >= 0
    sibling = (dp, chip * 2 + 1 - core)
    above = (dp, jnp.minimum(chip + 1, chips - 1) * 2 + core)
    below = (dp, jnp.maximum(chip - 1, 0) * 2 + core)
    load = pltpu.make_async_copy(tok_ref.at[pl.ds(dp * rows, rows)], mine_ref, tok_sem)
    load.start()
    greet(
        [(true, (lax.rem(dp + k, dp_size), ex)) for k in range(1, dp_size)]
        + [(true, sibling), (upper, above), (lower, below)]
    )
    copies = []
    for k in range(1, dp_size):
        peer = lax.rem(dp + k, dp_size)
        copy = send(
            proj_ref.at[pl.ds(peer * rows, rows)],
            got_ref.at[k - 1],
            rs_send.at[k - 1],
            rs_recv.at[k - 1],
            (peer, ex),
        )
        copy.start()
        copies.append(copy)
    load.wait()
    attn = proj_ref[pl.ds(dp * rows, rows), :].astype(jnp.float32)
    for k, copy in enumerate(copies):
        copy.wait()
        attn = attn + got_ref[k].astype(jnp.float32)
    stream = mine_ref[...].astype(jnp.float32) + attn
    stream_ref[...] = stream
    moe_in = rms_scale(stream, gain_ref[...]).astype(jnp.bfloat16)
    ext_ref[:, :width] = moe_in
    logits = mm(moe_in, router_ref[...])
    chosen = chosen_ref[...] > 0.0
    top = jnp.max(jnp.where(chosen, logits, neg_large), axis=-1, keepdims=True)
    weights = jnp.where(chosen, jnp.exp(jnp.where(chosen, logits, top) - top), 0.0)
    gates = weights / (0.5 * jnp.sum(weights, axis=-1, keepdims=True))
    half = gates.shape[1] // 2
    coarse = gates.astype(jnp.bfloat16).astype(jnp.float32)
    lane = lax.broadcasted_iota(jnp.int32, gates.shape, 1)
    ext_ref[:, width:] = jnp.where(lane < half, coarse, gates - coarse).astype(jnp.bfloat16)

    def block(chip_id, core_id):
        bounded = jnp.clip(chip_id, 0, chips - 1)
        return all_ref.at[pl.ds((bounded * 2 + core_id) * rows, rows)]

    own = pltpu.make_async_copy(ext_ref, block(chip, core), own_sem)
    own.start()

    def hop(chip_id, src, sends, recvs, index, target):
        return send(src, block(chip_id, core), sends.at[index], recvs.at[index], target)

    waits = []
    for s in range(chips):
        if s < chips - 1:
            for sign, edge, target, sends, recvs in (
                (-1, upper, above, up_send, up_recv),
                (1, lower, below, dn_send, dn_recv),
            ):
                origin = chip + sign * s
                cond = edge & (origin >= 0) & (origin < chips)
                copy = hop(origin, ext_ref if s == 0 else block(origin, core), sends, recvs, s, target)
                start_if(cond, copy)
                waits.append((cond, copy))
        for sign, index in ((-1, s), (1, chips - 1 + s)):
            origin = chip + sign * s
            if s == 0 and sign == 1:
                continue
            cond = (origin >= 0) & (origin < chips)
            copy = hop(origin, ext_ref if s == 0 else block(origin, core), sib_send, sib_recv, index, sibling)
            start_if(cond, copy)
            waits.append((cond, copy))
        if s < chips - 1:
            for sign, target, sends, recvs in (
                (-1, above, up_send, up_recv),
                (1, below, dn_send, dn_recv),
            ):
                origin = chip + sign * (s + 1)
                cond = (origin >= 0) & (origin < chips)
                copy = hop(origin, ext_ref, sends, recvs, s, target)
                pl.when(cond)(copy.wait_recv)
    for cond, copy in waits:
        pl.when(cond)(copy.wait_send)
    for s in range(chips):
        for sign, index in ((-1, s), (1, chips - 1 + s)):
            if s == 0 and sign == 1:
                continue
            origin = chip + sign * s
            copy = send(ext_ref, block(origin, 1 - core), sib_send.at[index], sib_recv.at[index], sibling)
            pl.when((origin >= 0) & (origin < chips))(copy.wait_recv)
    own.wait()


def exchange(projected, tokens, gain, router2, chosen2, dp_size, ex_size):
    group_rows, width = tokens.shape
    rows = group_rows // dp_size
    wide = width + router2.shape[1]
    chips = ex_size // 2
    dma = pltpu.SemaphoreType.DMA
    vmem = pl.BlockSpec(memory_space=pltpu.VMEM)
    hbm = pl.BlockSpec(memory_space=pl.ANY)
    return pl.pallas_call(
        functools.partial(exchange_kernel, dp_size, chips),
        out_shape=(
            jax.ShapeDtypeStruct((rows, width), jnp.float32),
            jax.ShapeDtypeStruct((ex_size * rows, wide), jnp.bfloat16),
        ),
        in_specs=[vmem, hbm, vmem, vmem, vmem],
        out_specs=(vmem, hbm),
        scratch_shapes=[
            pltpu.VMEM((rows, width), jnp.bfloat16),
            pltpu.VMEM((dp_size - 1, rows, width), jnp.bfloat16),
            pltpu.VMEM((rows, wide), jnp.bfloat16),
            dma,
            dma,
            dma((dp_size - 1,)),
            dma((dp_size - 1,)),
        ]
        + [dma((chips - 1,))] * 4
        + [dma((2 * chips - 1,))] * 2,
        compiler_params=pltpu.CompilerParams(
            collective_id=0, has_side_effects=True, vmem_limit_bytes=40 << 20
        ),
        name="exchange",
    )(projected, tokens, gain.reshape(1, width), router2, chosen2)


def collect_kernel(
    chips, part_ref, stream_ref, gain_ref, out_ref,
    sib_ref, sum_ref, up_ref, dn_ref,
    sib_send, sib_recv, up_send, up_recv, dn_send, dn_recv,
):
    rows = stream_ref.shape[0]
    dp, ex = lax.axis_index("dp"), lax.axis_index("expert")
    chip, core = ex // 2, ex % 2
    upper, lower = chip < chips - 1, chip > 0
    sibling = (dp, chip * 2 + 1 - core)
    above = (dp, jnp.minimum(chip + 1, chips - 1) * 2 + core)
    below = (dp, jnp.maximum(chip - 1, 0) * 2 + core)
    greet([(chip >= 0, sibling), (upper, above), (lower, below)])
    order = [k for pair in zip(range(chips), reversed(range(chips))) for k in pair][:chips]
    swaps = []
    for d in order:
        copy = send(
            part_ref.at[pl.ds((d * 2 + 1 - core) * rows, rows)],
            sib_ref.at[d],
            sib_send.at[d],
            sib_recv.at[d],
            sibling,
        )
        copy.start()
        swaps.append(copy)
    for d, copy in zip(order, swaps):
        copy.wait_recv()
        mine = part_ref[pl.ds((d * 2 + core) * rows, rows), :].astype(jnp.float32)
        sum_ref[d] = (mine + sib_ref[d].astype(jnp.float32)).astype(jnp.bfloat16)

    waits = []
    for s in range(1, chips):
        for index, (edge, target, buf, sends, recvs) in enumerate(
            ((lower, below, dn_ref, dn_send, dn_recv), (upper, above, up_ref, up_send, up_recv))
        ):
            place = chips - 1 - chip if index == 0 else chip
            hop = s - 1 - place
            dest = hop if index == 0 else chips - 1 - hop
            bounded = jnp.clip(dest, 0, chips - 1)
            valid = edge & (hop >= 0) & ((dest < chip) if index == 0 else (dest > chip))
            copy = send(
                sum_ref.at[bounded], buf.at[s - 1], sends.at[s - 1], recvs.at[s - 1], target
            )
            if s > 1:

                @pl.when(valid & (place > 0))
                def _():
                    total = sum_ref[bounded].astype(jnp.float32)
                    total = total + buf[s - 2].astype(jnp.float32)
                    sum_ref[bounded] = total.astype(jnp.bfloat16)

            start_if(valid, copy)
            waits.append((valid, copy))
        for index, (edge, target, buf, sends, recvs) in enumerate(
            ((upper, below, dn_ref, dn_send, dn_recv), (lower, above, up_ref, up_send, up_recv))
        ):
            place = chips - 1 - chip if index == 0 else chip
            hop = s - place
            dest = hop if index == 0 else chips - 1 - hop
            valid = edge & (hop >= 0) & ((dest <= chip) if index == 0 else (dest >= chip))
            copy = send(sum_ref.at[0], buf.at[s - 1], sends.at[s - 1], recvs.at[s - 1], target)
            pl.when(valid)(copy.wait_recv)
    last = chips - 2
    total = stream_ref[...] + sum_ref[chip].astype(jnp.float32)
    total = total + jnp.where(upper, dn_ref[last].astype(jnp.float32), 0.0)
    total = total + jnp.where(lower, up_ref[last].astype(jnp.float32), 0.0)
    out_ref[...] = rms_scale(total, gain_ref[...]).astype(jnp.bfloat16)
    for cond, copy in waits:
        pl.when(cond)(copy.wait_send)
    for copy in swaps:
        copy.wait_send()


def collect(partial, stream, gain, ex_size):
    rows, width = stream.shape
    chips = ex_size // 2
    dma = pltpu.SemaphoreType.DMA
    vmem = pl.BlockSpec(memory_space=pltpu.VMEM)
    blocks = pltpu.VMEM((chips, rows, width), jnp.bfloat16)
    landing = pltpu.VMEM((chips - 1, rows, width), jnp.bfloat16)
    return pl.pallas_call(
        functools.partial(collect_kernel, chips),
        out_shape=jax.ShapeDtypeStruct((rows, width), jnp.bfloat16),
        in_specs=[vmem] * 3,
        out_specs=vmem,
        scratch_shapes=[blocks, blocks, landing, landing, dma((chips,)), dma((chips,))]
        + [dma((chips - 1,))] * 4,
        compiler_params=pltpu.CompilerParams(
            collective_id=1, has_side_effects=True, vmem_limit_bytes=56 << 20
        ),
        name="collect",
    )(partial, stream, gain.reshape(1, width))


def experts_kernel(
    span, me_ref, ext_ref, win_ref, wout_ref, out_ref, rank_ref, rank_t_ref, acc_ref
):
    s = pl.program_id(0)
    slots = pl.num_programs(0)
    rows, wide = ext_ref.shape
    width = acc_ref.shape[1]
    extra = wide - width
    ff_width = wout_ref.shape[1]
    first = me_ref[0] * slots

    def pick_slot(shape, dim_from, dim_to, offset):
        source = lax.broadcasted_iota(jnp.int32, shape, dim_from) % (extra // 2)
        target = lax.broadcasted_iota(jnp.int32, shape, dim_to)
        return source == target + offset

    @pl.when(s == 0)
    def _():
        choose = pick_slot((extra, 128), 0, 1, first) & (
            lax.broadcasted_iota(jnp.int32, (extra, 128), 1) < slots
        )
        choose = jnp.where(choose, 1.0, 0.0).astype(jnp.bfloat16)
        before = jnp.where(
            lax.broadcasted_iota(jnp.int32, (span, span), 1)
            < lax.broadcasted_iota(jnp.int32, (span, span), 0),
            1.0,
            0.0,
        ).astype(jnp.bfloat16)
        seen = jnp.zeros((1, 128), jnp.float32)
        for part in range(rows // span):
            here = slice(part * span, (part + 1) * span)
            used = mm(ext_ref[here, width:], choose) > 0.0
            ones = jnp.where(used, 1.0, 0.0)
            rank = mm(before, ones.astype(jnp.bfloat16)) + seen
            rank = jnp.where(used, rank, -1.0)
            seen = seen + jnp.sum(ones, axis=0, keepdims=True)
            rank_ref[here, :] = rank
            rank_t_ref[:, here] = rank.T[: rank_t_ref.shape[0], :]
        acc_ref[...] = jnp.zeros_like(acc_ref)

    rank_row = rank_t_ref[pl.ds(s, 1), :]
    count = jnp.max(rank_row).astype(jnp.int32) + 1
    chunk = math.gcd(rows, 512)
    tile_rows = 320 if rows <= MOST_ROWS else 64

    def tile(index, carried):
        base = (index * tile_rows).astype(jnp.float32)
        wanted = base + lax.broadcasted_iota(jnp.int32, (tile_rows, rows), 0).astype(jnp.float32)
        select = jnp.where(wanted == rank_row, 1.0, 0.0).astype(jnp.bfloat16)
        taken = mm(select, ext_ref[...])
        moe_in = taken[:, :width].astype(jnp.bfloat16)
        lane = lax.broadcasted_iota(jnp.int32, (tile_rows, extra), 1) % (extra // 2)
        mine = lane == first + s
        gate = jnp.sum(jnp.where(mine, taken[:, width:], 0.0), axis=1, keepdims=True)
        gate_up = mm(moe_in, win_ref[0])
        g = gate_up[:, :ff_width]
        activation = (g / (1.0 + jnp.exp(-g)) * gate_up[:, ff_width:]).astype(jnp.bfloat16)
        produced = (mm(activation, wout_ref[0]) * gate).astype(jnp.bfloat16)
        for part in range(rows // chunk):
            here = slice(part * chunk, (part + 1) * chunk)
            lane_id = lax.broadcasted_iota(jnp.int32, (chunk, 128), 1)
            column = jnp.sum(
                jnp.where(lane_id == s, rank_ref[here, :], 0.0), axis=1, keepdims=True
            )
            place = base + lax.broadcasted_iota(jnp.int32, (chunk, tile_rows), 1).astype(jnp.float32)
            spread = jnp.where(place == column, 1.0, 0.0).astype(jnp.bfloat16)
            acc_ref[here, :] = acc_ref[here, :] + mm(spread, produced)
        return carried

    lax.fori_loop(0, (count + tile_rows - 1) // tile_rows, tile, 0)

    @pl.when(s == slots - 1)
    def _():
        out_ref[...] = acc_ref[...].astype(jnp.bfloat16)


def run_experts(me, gathered, expert_in, expert_out, span):
    rows, wide = gathered.shape
    slots, width, double = expert_in.shape
    ff_width = expert_out.shape[1]
    return pl.pallas_call(
        functools.partial(experts_kernel, span),
        out_shape=jax.ShapeDtypeStruct((rows, width), jnp.bfloat16),
        grid_spec=pltpu.PrefetchScalarGridSpec(
            num_scalar_prefetch=1,
            grid=(slots,),
            in_specs=[
                pl.BlockSpec((rows, wide), lambda i, me: (0, 0), pipeline_mode=pl.Buffered(1)),
                pl.BlockSpec((1, width, double), lambda i, me: (i, 0, 0)),
                pl.BlockSpec((1, ff_width, width), lambda i, me: (i, 0, 0)),
            ],
            out_specs=pl.BlockSpec((rows, width), lambda i, me: (0, 0), pipeline_mode=pl.Buffered(1)),
            scratch_shapes=[
                pltpu.VMEM((rows, 128), jnp.float32),
                pltpu.VMEM((-(-slots // 8) * 8, rows), jnp.float32),
                pltpu.VMEM((rows, width), jnp.float32),
            ],
        ),
        compiler_params=pltpu.CompilerParams(vmem_limit_bytes=64000 << 10),
        name="run_experts",
    )(me, gathered, expert_in, expert_out)


def choose_slots(slot_owner, routes, split_pick):
    slot_ids = jnp.arange(slot_owner.shape[0], dtype=jnp.int32)
    same_owner = slot_owner[:, None] == slot_owner[None, :]
    slot_rank = jnp.sum(
        (same_owner & (slot_ids[None, :] < slot_ids[:, None])).astype(jnp.int32), axis=1
    )
    replicas = jnp.sum(same_owner.astype(jnp.int32), axis=1)
    hits = (slot_owner[None, None, :] == routes[:, :, None]) & (
        slot_rank[None, None, :] == split_pick[:, :, None] % replicas[None, None, :]
    )
    return jnp.any(hits, axis=1).astype(jnp.float32)


def shards(
    tokens,
    past_len,
    cache_keys,
    cache_values,
    attn_gain,
    w_query,
    w_key,
    w_value,
    w_out,
    moe_gain,
    router,
    expert_in,
    expert_out,
    final_gain,
    slot_owner,
    routes,
    split_pick,
):
    chosen = choose_slots(slot_owner, routes, split_pick)
    chosen2 = jnp.concatenate([chosen, chosen], axis=1)
    owner2 = jnp.concatenate([slot_owner, slot_owner])
    pick = owner2[None, :] == jnp.arange(router.shape[1], dtype=jnp.int32)[:, None]
    router2 = mm(router, pick.astype(jnp.bfloat16)).astype(jnp.bfloat16)
    projected = attend(
        past_len, tokens, attn_gain, w_query, w_key, w_value, w_out, cache_keys, cache_values
    )
    dp_size, ex_size = lax.axis_size("dp"), lax.axis_size("expert")
    tok_dev = tokens.shape[0] // dp_size
    stream, gathered = exchange(
        projected, tokens, moe_gain, router2, chosen2, dp_size, ex_size
    )
    me = lax.axis_index("expert").astype(jnp.int32).reshape(1)
    partial = run_experts(me, gathered, expert_in, expert_out, tok_dev)
    return collect(partial, stream, final_gain, ex_size)


def solution(mesh):
    return jax.shard_map(
        shards,
        mesh=mesh,
        in_specs=(
            P("expert", None),
            P("expert"),
            P("expert", None, "dp"),
            P("expert", None, "dp"),
            P(),
            P(None, "dp"),
            P(None, "dp"),
            P(None, "dp"),
            P("dp", None),
            P(),
            P(),
            P("expert", None, None),
            P("expert", None, None),
            P(),
            P(),
            P(("expert", "dp"), None),
            P(("expert", "dp"), None),
        ),
        out_specs=P(("expert", "dp"), None),
        check_vma=False,
    )
```
